32 devices in a mesh: tok: 4 (over z), col: 8 (over y, x, core).
Axes of the slice: x: 2, y: 2, z: 4, core: 2. Of those that a mesh axis runs over, the one named last changes fastest.
Arguments:
- activations: bfloat16 [1024, 4096], P('tok'), may hold values from -6 to 6
- out_grad: bfloat16 [1024, 8192], P('tok', 'col'), may hold values from -0.1875 to 0.1875
- owned_blocks: int32 [4, 8, 5], P('tok'), may hold values from -1 to 127, as said below
- gram_left: float32 [4, 8, 5, 512, 512], P('tok', 'col'), may hold values from -6144 to 6656, as said below
- gram_right: float32 [4, 8, 5, 512, 512], P('tok', 'col'), may hold values from -6144 to 6656, as said below
Outputs:
- precond: bfloat16 [4096, 8192], P('tok', 'col')
- left_new: float32 [4, 8, 5, 512, 512], P('tok', 'col')
- right_new: float32 [4, 8, 5, 512, 512], P('tok', 'col')
The draws below stay inside these ranges and needn't reach their ends.
Inputs may be any that keep to these rules, and one draw needn't show every extreme that they name: owned_blocks[t] lists every block whose rows lie in rows t * 2 * 512 to (t + 1) * 2 * 512 - 1 exactly once; each device lists its block ids in ascending order followed by -1; the blocks of one device lie in pairwise different block columns; in each t some device fills all 5 slots. `gram_left`: each slot holds a symmetric positive definite matrix with eigenvalues of at least 256. `gram_right`: each slot holds a symmetric positive definite matrix with eigenvalues of at least 256.
All inputs are finite; a program needn't handle non-finite values.
Results may differ from the reference program's by a relative error of at most 0.015.
Values may be sent and summed in bfloat16 or wider, within the bound.
A program may use at most 128 MiB of HBM per device.

```python
import jax
import jax.numpy as jnp
from jax import lax

D = 8192
DI = 4096
B = 512
ITERS = 2
TOKENS = 1024
COL_BLOCKS = 16
ROW_BLOCKS = 2
SLOTS = 5
N_TOK = 4
N_COL = 8


def group_owners(key, group_index):
    mean_load = ROW_BLOCKS * COL_BLOCKS // N_COL
    spare_slots = SLOTS - mean_load
    sentinel = N_TOK * ROW_BLOCKS * COL_BLOCKS
    subkeys = jax.random.split(key, 4)
    lift_sizes = jax.random.randint(subkeys[0], (N_COL // 2,), 0, spare_slots + 1)
    lift_sizes = lift_sizes.at[0].set(spare_slots)
    load_counts = jnp.concatenate([mean_load - lift_sizes, mean_load + lift_sizes])
    load_counts = load_counts[jax.random.permutation(subkeys[1], N_COL)]
    starts = jnp.cumsum(load_counts) - load_counts
    positions = jnp.arange(SLOTS)
    rank_table = jnp.minimum(starts[:, None] + positions[None, :], ROW_BLOCKS * COL_BLOCKS - 1)
    filled = positions[None, :] < load_counts[:, None]
    row_order = jax.random.permutation(subkeys[2], ROW_BLOCKS)
    col_order = jax.random.permutation(subkeys[3], COL_BLOCKS)
    block_ids = (group_index * ROW_BLOCKS + row_order[rank_table // COL_BLOCKS]) * COL_BLOCKS + col_order[rank_table % COL_BLOCKS]
    marked = jnp.where(filled, block_ids, sentinel)
    ordered = jnp.sort(marked, axis=1)
    return jnp.where(ordered >= sentinel, -1, ordered).astype(jnp.int32)


def draw_owned_blocks(key, part):
    return jnp.stack([group_owners(jax.random.fold_in(key, 101 + group_index), group_index) for group_index in range(N_TOK)])


def gram_draw(key):
    total = N_TOK * N_COL * SLOTS

    def one_matrix(subkey):
        factor = jax.random.normal(subkey, (B, B), jnp.float32)
        product = jnp.dot(factor, factor.T, precision=lax.Precision.HIGHEST)
        return product + 0.5 * B * jnp.eye(B, dtype=jnp.float32)
    matrices = lax.map(one_matrix, jax.random.split(key, total))
    return matrices.reshape(N_TOK, N_COL, SLOTS, B, B)


def draw_gram_left(key, part):
    return gram_draw(jax.random.fold_in(key, 11))


def draw_gram_right(key, part):
    return gram_draw(jax.random.fold_in(key, 23))


def block_scale(key, shape, shards, smallest, high):
    loudness, own = 1.0, jax.random.fold_in(key, 6)
    for axis_at, shards_of in shards:
        steps = jnp.exp(jax.random.uniform(jax.random.fold_in(own, axis_at), (shards_of,), jnp.float32, smallest / len(shards), high / len(shards)))
        loudness = loudness * jnp.repeat(steps, shape[axis_at] // shards_of).reshape([-1 if axis == axis_at else 1 for axis in range(len(shape))])
    return loudness


def noise(key, extent, scale, reach, cuts=(), kind=jnp.bfloat16):
    drawn = scale * jax.random.normal(key, extent, jnp.float32)
    if cuts:
        drawn = drawn * block_scale(key, extent, cuts, -0.22, 0.18)
    return jnp.clip(drawn, -reach, reach).astype(kind)


def setup_inputs(seed: int = 0) -> dict:
    key_of = jax.random.split(jax.random.key(seed), 6)
    activations = noise(key_of[0], (TOKENS, DI), 1.0, 6.0, ((0, 4),))
    out_grad = noise(key_of[1], (TOKENS, D), TOKENS ** -0.5, 0.1875, ((0, 4), (1, 8)))
    owned_blocks = draw_owned_blocks(jax.random.fold_in(key_of[5], 71), 0)
    gram_left = draw_gram_left(jax.random.fold_in(key_of[5], 71), 0)
    gram_right = draw_gram_right(jax.random.fold_in(key_of[5], 71), 0)
    return {"activations": activations, "out_grad": out_grad, "owned_blocks": owned_blocks, "gram_left": gram_left, "gram_right": gram_right}


highest = lax.Precision.HIGHEST
decay_rate = 0.9
epsilon = 1e-06

def inverse_root(matrix):
    side = matrix.shape[-1]
    identity = jnp.eye(side, dtype=jnp.float32)
    mean_diag = jnp.trace(matrix, axis1=-2, axis2=-1) / side
    coupled = matrix / mean_diag[..., None, None]
    root = identity
    for iteration in range(ITERS):
        factor = (5.0 * identity - coupled) * 0.25
        if iteration == 0:
            root = factor
        else:
            root = jnp.einsum('...ij,...jk->...ik', root, factor, precision=highest)
        if iteration + 1 < ITERS:
            squared = jnp.einsum('...ij,...jk->...ik', factor, factor, precision=highest)
            fourth = jnp.einsum('...ij,...jk->...ik', squared, squared, precision=highest)
            coupled = jnp.einsum('...ij,...jk->...ik', fourth, coupled, precision=highest)
    return root

def reference(activations, out_grad, owned_blocks, gram_left, gram_right):
    gradient = jnp.dot(activations.T, out_grad, preferred_element_type=jnp.float32).astype(jnp.bfloat16)
    col_blocks = D // B
    block_ids = owned_blocks.reshape(-1).astype(jnp.int32)
    lefts = gram_left.reshape(-1, B, B)
    rights = gram_right.reshape(-1, B, B)

    def per_slot(inputs):
        ident, left_old, right_old = inputs
        occupied = ident >= 0
        clamped = jnp.where(occupied, ident, 0)
        row_start = (clamped // col_blocks * B).astype(jnp.int32)
        col_start = (clamped % col_blocks * B).astype(jnp.int32)
        block = lax.dynamic_slice(gradient, (row_start, col_start), (B, B))
        grad_block = jnp.where(occupied, block.astype(jnp.float32), jnp.float32(0.0))
        left_next = jnp.where(occupied, decay_rate * left_old + jnp.dot(grad_block, grad_block.T, precision=highest), left_old)
        right_next = jnp.where(occupied, decay_rate * right_old + jnp.dot(grad_block.T, grad_block, precision=highest), right_old)
        root_left = inverse_root(left_next)
        root_right = inverse_root(right_next)
        shaped = jnp.dot(jnp.dot(root_left, grad_block, precision=highest), root_right, precision=highest)
        grad_norm = jnp.sqrt(jnp.sum(grad_block * grad_block) + epsilon)
        shaped_norm = jnp.sqrt(jnp.sum(shaped * shaped) + epsilon)
        result = (shaped * (grad_norm / shaped_norm)).astype(jnp.bfloat16)
        return (left_next, right_next, result)
    left_all, right_all, results = lax.map(per_slot, (block_ids, lefts, rights))

    def place(index, canvas):
        ident = block_ids[index]
        occupied = ident >= 0
        clamped = jnp.where(occupied, ident, 0)
        row_start = (clamped // col_blocks * B).astype(jnp.int32)
        col_start = (clamped % col_blocks * B).astype(jnp.int32)
        present = lax.dynamic_slice(canvas, (row_start, col_start), (B, B))
        update = jnp.where(occupied, results[index], present)
        return lax.dynamic_update_slice(canvas, update, (row_start, col_start))
    precond = lax.fori_loop(0, block_ids.shape[0], place, jnp.zeros((DI, D), jnp.bfloat16))
    return (precond, left_all.reshape(gram_left.shape), right_all.reshape(gram_right.shape))
```

```python
import jax
import jax.numpy as jnp
from jax import lax
from jax.sharding import PartitionSpec as P

B = 512
decay_rate = 0.9
epsilon = 1e-06
f32 = jnp.float32
bf16 = jnp.bfloat16


def mm(a, b):
    return jnp.einsum("sij,sjk->sik", a.astype(bf16), b.astype(bf16), preferred_element_type=f32)


def root_minus_identity(matrix):
    side = matrix.shape[-1]
    identity = jnp.eye(side, dtype=f32)
    mean_diag = jnp.trace(matrix, axis1=-2, axis2=-1) / side
    e = (identity - matrix / mean_diag[..., None, None]) * 0.25
    w = 2.0 * e + mm(e, e)
    v = w + e + mm(e, w)
    r = v - 1.25 * w
    return 1.25 * e + r - 0.25 * v + mm(v, r)


def per_device(activations, out_grad, owned_blocks, gram_left, gram_right):
    tok_count = lax.axis_size("tok")
    col_count = lax.axis_size("col")
    tok_index = lax.axis_index("tok")
    col_index = lax.axis_index("col")
    tok_local, shard_width = out_grad.shape
    rows_home = activations.shape[1] // tok_count
    row_blocks = rows_home // B
    col_blocks = shard_width * col_count // B
    piece_width = min(B, shard_width)
    per_home = shard_width // piece_width
    per_block = B // piece_width
    sub = piece_width // col_count
    part = per_block * sub
    owners = owned_blocks[0]
    slots = owners.shape[1]

    og = out_grad.T.reshape(per_home, col_count, sub, tok_local).transpose(1, 0, 2, 3)
    og = lax.all_to_all(og, "col", split_axis=0, concat_axis=0, tiled=True)
    og = og.reshape(col_count * per_home * sub, tok_local)
    og = lax.all_gather(og, "tok", axis=1, tiled=True)
    act = lax.all_to_all(activations, "tok", split_axis=1, concat_axis=0, tiled=True)
    grad = jnp.dot(og, act, preferred_element_type=f32).astype(bf16)

    grad = grad.reshape(col_blocks, part, row_blocks, B)
    live = owners >= 0
    ids = jnp.where(live, owners, tok_index * row_blocks * col_blocks)
    send = grad[ids % col_blocks, :, ids // col_blocks - tok_index * row_blocks]
    got = lax.all_to_all(send, "col", split_axis=0, concat_axis=0, tiled=True)
    got = got.reshape(col_count, slots, per_block, sub, B).transpose(1, 2, 0, 3, 4)
    gt = got.reshape(slots, B, B)

    mine = lax.dynamic_index_in_dim(owners, col_index, 0, keepdims=False) >= 0
    mine = mine[:, None, None]
    gt = jnp.where(mine, gt, jnp.zeros((), bf16))
    left_old = gram_left[0, 0]
    right_old = gram_right[0, 0]
    left = jnp.einsum("sji,sjk->sik", gt, gt, preferred_element_type=f32)
    right = jnp.einsum("sij,skj->sik", gt, gt, preferred_element_type=f32)
    left_next = jnp.where(mine, decay_rate * left_old + left, left_old)
    right_next = jnp.where(mine, decay_rate * right_old + right, right_old)
    yl = root_minus_identity(left_next)
    yr = root_minus_identity(right_next)
    g32 = gt.astype(f32)
    first = g32 + mm(yr, gt)
    shaped = first + mm(first, yl)
    grad_norm = jnp.sqrt(jnp.sum(g32 * g32, axis=(1, 2)) + epsilon)
    shaped_norm = jnp.sqrt(jnp.sum(shaped * shaped, axis=(1, 2)) + epsilon)
    result = (shaped * (grad_norm / shaped_norm)[:, None, None]).astype(bf16)

    back = result.reshape(slots, per_block, col_count, sub, B).transpose(2, 0, 1, 3, 4)
    back = back.reshape(col_count, slots, part, B)
    back = lax.all_to_all(back, "col", split_axis=0, concat_axis=0, tiled=True)
    back = back.reshape(col_count * slots, per_block, sub, B)
    home = jnp.arange(col_count * per_home)
    wanted = (tok_index * row_blocks + jnp.arange(row_blocks))[None, :] * col_blocks + (
        home // per_block
    )[:, None]
    match = owners.reshape(-1)[None, None, :] == wanted[:, :, None]
    pick = jnp.argmax(match, axis=2)
    out = back[pick, (home % per_block)[:, None]]
    out = out.reshape(col_count, per_home, row_blocks, sub, B)
    out = lax.all_to_all(out, "col", split_axis=0, concat_axis=0, tiled=True)
    out = out.transpose(2, 4, 1, 0, 3).reshape(rows_home, shard_width)
    return (out, left_next[None, None], right_next[None, None])


def solution(mesh):
    in_specs = (
        P("tok", None),
        P("tok", "col"),
        P("tok", None, None),
        P("tok", "col", None, None, None),
        P("tok", "col", None, None, None),
    )
    out_specs = (
        P("tok", "col"),
        P("tok", "col", None, None, None),
        P("tok", "col", None, None, None),
    )
    return jax.shard_map(
        per_device, mesh=mesh, in_specs=in_specs, out_specs=out_specs, check_vma=False
    )
```

```python
import functools

import jax
import jax.numpy as jnp
from jax import lax
from jax.experimental import pallas as pl
from jax.experimental.pallas import tpu as pltpu
from jax.sharding import PartitionSpec as P

B = 512
decay_rate = 0.9
epsilon = 1e-06
f32 = jnp.float32
bf16 = jnp.bfloat16
MESH = pl.DeviceIdType.MESH
VMEM = pl.BlockSpec(memory_space=pltpu.VMEM)
ANY = pl.BlockSpec(memory_space=pl.ANY)
LIMIT = 60 * 1024 * 1024


def mm(a, b):
    return jnp.dot(a.astype(bf16), b.astype(bf16), preferred_element_type=f32)


def gather_kernel(tok_count, col_count, og_ref, act_ref, og_buf, act_buf, sems, local_sems):
    t = lax.axis_index("tok")
    c = lax.axis_index("col")
    core = lax.rem(c, 2)
    chip = c // 2
    chips = col_count // 2
    partner = chip * 2 + 1 - core
    width = act_buf.shape[3]

    barrier = pltpu.get_barrier_semaphore()
    for d in range(1, col_count):
        pl.semaphore_signal(
            barrier, inc=1, device_id=(t, lax.rem(c + d, col_count)), device_id_type=MESH
        )
    for d in range(1, tok_count):
        pl.semaphore_signal(
            barrier, inc=1, device_id=(lax.rem(t + d, tok_count), c), device_id_type=MESH
        )

    def act_piece(to):
        return act_ref.at[c, :, pl.ds(pl.multiple_of(to * width, width), width)]

    own_act = pltpu.make_async_copy(act_piece(t), act_buf.at[t, c], local_sems.at[0])
    own_act.start()
    own_og = pltpu.make_async_copy(og_ref.at[c], og_buf.at[t, c], local_sems.at[1])
    own_og.start()
    pl.semaphore_wait(barrier, col_count + tok_count - 2)

    def remote(src, dst, kind, sent, received, to):
        return pltpu.make_async_remote_copy(
            src_ref=src,
            dst_ref=dst,
            send_sem=sems.at[kind, 0, sent],
            recv_sem=sems.at[kind, 1, received],
            device_id=to,
            device_id_type=MESH,
        )

    sent = []
    for d in range(1, tok_count):
        to = lax.rem(t + d, tok_count)
        copy = remote(act_piece(to), act_buf.at[t, c], 0, d, t, (to, c))
        copy.start()
        sent.append(copy)
    for d in range(1, col_count):
        to = lax.rem(c + d, col_count)
        copy = remote(og_ref.at[to], og_buf.at[t, c], 1, d, c, (t, to))
        copy.start()
        sent.append(copy)

    for d in range(1, col_count):
        source = lax.rem(c + d, col_count)
        remote(og_buf.at[t, source], og_buf.at[t, source], 1, d, source, (t, source)).wait_recv()
    own_og.wait()

    def pass_on(origin, step, kind):
        to = t + step
        return remote(og_buf.at[origin], og_buf.at[origin], kind, origin, origin, (to, c))

    @pl.when(t < tok_count - 1)
    def _():
        pass_on(t, 1, 2).start()

    @pl.when(t > 0)
    def _():
        pass_on(t, -1, 3).start()

    own_act.wait()
    for d in range(1, tok_count):
        source = lax.rem(t + d, tok_count)
        remote(act_buf.at[source, c], act_buf.at[source, c], 0, d, source, (source, c)).wait_recv()

    def share(piece, kind, sem_sent, sem_received, to):
        return remote(
            act_buf.at[:, piece], act_buf.at[:, piece], kind, sem_sent, sem_received, (t, to)
        )

    for d in range(1, chips):
        to = lax.rem(chip + d, chips) * 2 + core
        copy = share(c, 4, d, chip, to)
        copy.start()
        sent.append(copy)
    copy = share(c, 5, 0, chip, partner)
    copy.start()
    sent.append(copy)

    def relay(origin, step, kind):
        pass_on(origin, -step, kind).wait_recv()

        @pl.when((t + step >= 0) & (t + step < tok_count))
        def _():
            pass_on(origin, step, kind).start()

    for d in range(1, chips):
        other = lax.rem(chip + d, chips)
        piece = other * 2 + core
        share(piece, 4, d, other, piece).wait_recv()
        copy = share(piece, 5, d, other, partner)
        copy.start()
        sent.append(copy)

    for d in range(1, tok_count):

        @pl.when(t - d >= 0)
        def _():
            relay(t - d, 1, 2)

        @pl.when(t + d < tok_count)
        def _():
            relay(t + d, -1, 3)

    for d in range(chips):
        other = lax.rem(chip + d, chips)
        piece = other * 2 + 1 - core
        share(piece, 5, d, other, partner).wait_recv()
    for copy in sent:
        copy.wait_send()
    for origin in range(tok_count):

        @pl.when((t >= origin) & (t < tok_count - 1))
        def _():
            pass_on(origin, 1, 2).wait_send()

        @pl.when((t <= origin) & (t > 0))
        def _():
            pass_on(origin, -1, 3).wait_send()


def grad_kernel(table, og_ref, act_ref, send_ref, grad, *, slots, row_blocks, col_count):
    tok_count = og_ref.shape[0]
    col_blocks, part = grad.shape[1:3]
    base = lax.axis_index("tok") * (row_blocks * col_blocks)
    step = 256
    blocks = step // part

    @pl.loop(0, col_blocks // blocks)
    def _(i):
        rows = pl.ds(pl.multiple_of(i * step, step), step)
        total = sum(
            jnp.dot(og_ref[t, rows], act_ref[t], preferred_element_type=f32)
            for t in range(tok_count)
        ).astype(bf16)
        for r in range(row_blocks):
            grad[r, pl.ds(i * blocks, blocks)] = total[:, r * B : (r + 1) * B].reshape(
                blocks, part, B
            )

    @pl.loop(0, col_count)
    def _(o):
        for s in range(slots):
            place = jnp.maximum(table[o * slots + s] - base, 0)
            send_ref[o, s] = grad[place // col_blocks, lax.rem(place, col_blocks)]


def root_minus_identity(matrix, diagonal):
    side = matrix.shape[-1]
    scale = 0.25 * side / jnp.sum(jnp.where(diagonal, matrix, 0.0))
    e = jnp.where(diagonal, 0.25, 0.0) - matrix * scale
    eb = e.astype(bf16)
    w = 2.0 * e + mm(eb, eb)
    v = w + e + mm(eb, w)
    r = v - 1.25 * w
    return (1.25 * e + r - 0.25 * v + mm(v, r)).astype(bf16)


def slot_kernel(live_ref, got_ref, left_ref, right_ref, back_ref, left_out, right_out):
    live = live_ref[pl.program_id(0)] > 0
    gt = got_ref[...].reshape(B, B)
    gt = jnp.where(live, gt, jnp.zeros_like(gt))
    g = gt.T
    rows = lax.broadcasted_iota(jnp.int32, (B, B), 0)
    cols = lax.broadcasted_iota(jnp.int32, (B, B), 1)
    diagonal = rows == cols
    decay = jnp.where(live, decay_rate, 1.0)
    left = decay * left_ref[0] + jnp.dot(g, gt, preferred_element_type=f32)
    right = decay * right_ref[0] + jnp.dot(gt, g, preferred_element_type=f32)
    left_out[0] = left
    right_out[0] = right
    yl = root_minus_identity(left, diagonal)
    yr = root_minus_identity(right, diagonal)
    g32 = gt.astype(f32)
    first = g32 + jnp.dot(yr, gt, preferred_element_type=f32)
    shaped = first + mm(first, yl)
    grad_norm = jnp.sqrt(jnp.sum(g32 * g32, keepdims=True) + epsilon)
    shaped_norm = jnp.sqrt(jnp.sum(shaped * shaped, keepdims=True) + epsilon)
    result = (shaped * (grad_norm / shaped_norm)).astype(bf16)
    back_ref[...] = result.reshape(back_ref.shape)


def place_kernel(in_ref, out_ref):
    width = out_ref.shape[1]
    out_ref[...] = in_ref[...].reshape(width, B).T


def per_device(activations, out_grad, owned_blocks, gram_left, gram_right):
    tok_count = lax.axis_size("tok")
    col_count = lax.axis_size("col")
    tok_index = lax.axis_index("tok")
    col_index = lax.axis_index("col")
    tok_local, shard_width = out_grad.shape
    rows_home = activations.shape[1] // tok_count
    row_blocks = rows_home // B
    col_blocks = shard_width * col_count // B
    piece_width = min(B, shard_width)
    per_home = shard_width // piece_width
    per_block = B // piece_width
    sub = piece_width // col_count
    part = per_block * sub
    owners = owned_blocks[0]
    slots = owners.shape[1]

    og = out_grad.T.reshape(per_home, col_count, sub, tok_local).transpose(1, 0, 2, 3)
    og = og.reshape(col_count, per_home * sub, tok_local)
    act = activations.reshape(col_count, tok_local // col_count, activations.shape[1])
    og, act = pl.pallas_call(
        functools.partial(gather_kernel, tok_count, col_count),
        out_shape=[
            jax.ShapeDtypeStruct((tok_count, col_count, per_home * sub, tok_local), bf16),
            jax.ShapeDtypeStruct(
                (tok_count, col_count, tok_local // col_count, rows_home), bf16
            ),
        ],
        in_specs=[ANY, ANY],
        out_specs=[VMEM, VMEM],
        scratch_shapes=[
            pltpu.SemaphoreType.DMA((6, 2, max(col_count, tok_count))),
            pltpu.SemaphoreType.DMA((2,)),
        ],
        compiler_params=pltpu.CompilerParams(
            collective_id=0, has_side_effects=True, vmem_limit_bytes=LIMIT // 4
        ),
    )(og, act)
    og = og.reshape(tok_count, col_count * per_home * sub, tok_local)
    act = act.reshape(tok_count, tok_local, rows_home)

    send = pl.pallas_call(
        functools.partial(
            grad_kernel, slots=slots, row_blocks=row_blocks, col_count=col_count
        ),
        out_shape=jax.ShapeDtypeStruct((col_count, slots, part, B), bf16),
        in_specs=[pl.BlockSpec(memory_space=pltpu.SMEM), VMEM, VMEM],
        out_specs=VMEM,
        scratch_shapes=[pltpu.VMEM((row_blocks, col_blocks, part, B), bf16)],
        compiler_params=pltpu.CompilerParams(vmem_limit_bytes=LIMIT // 2),
    )(owners.reshape(-1), og, act)
    got = lax.all_to_all(send, "col", split_axis=0, concat_axis=0, tiled=True)
    if per_block > 1:
        got = got.reshape(col_count, slots, per_block, sub, B).transpose(2, 0, 3, 1, 4)
        got = got.reshape(col_count, part, slots, B).transpose(0, 2, 1, 3)

    mine = lax.dynamic_index_in_dim(owners, col_index, 0, keepdims=False) >= 0
    square = pl.BlockSpec((1, B, B), lambda s, live: (s, 0, 0))
    pieces = pl.BlockSpec((col_count, 1, part, B), lambda s, live: (0, s, 0, 0))
    back, left_next, right_next = pl.pallas_call(
        slot_kernel,
        out_shape=[
            jax.ShapeDtypeStruct((col_count, slots, part, B), bf16),
            jax.ShapeDtypeStruct((slots, B, B), f32),
            jax.ShapeDtypeStruct((slots, B, B), f32),
        ],
        grid_spec=pltpu.PrefetchScalarGridSpec(
            num_scalar_prefetch=1,
            grid=(slots,),
            in_specs=[pieces, square, square],
            out_specs=[pieces, square, square],
        ),
        compiler_params=pltpu.CompilerParams(vmem_limit_bytes=LIMIT),
    )(mine.astype(jnp.int32), got, gram_left[0, 0], gram_right[0, 0])

    if per_block > 1:
        back = back.transpose(1, 0, 2, 3).reshape(slots, per_block, col_count, sub, B)
        back = back.transpose(2, 0, 1, 3, 4).reshape(col_count, slots, part, B)
    back = lax.all_to_all(back, "col", split_axis=0, concat_axis=0, tiled=True)
    back = back.reshape(col_count * slots, per_block, sub, B)
    home = jnp.arange(col_count * per_home)
    wanted = (tok_index * row_blocks + jnp.arange(row_blocks))[None, :] * col_blocks + (
        home // per_block
    )[:, None]
    match = owners.reshape(-1)[None, None, :] == wanted[:, :, None]
    pick = jnp.argmax(match, axis=2)
    out = back[pick, (home % per_block)[:, None]]
    out = out.reshape(col_count, per_home, row_blocks, sub, B)
    out = lax.all_to_all(out, "col", split_axis=0, concat_axis=0, tiled=True)
    out = pl.pallas_call(
        place_kernel,
        out_shape=jax.ShapeDtypeStruct((rows_home, shard_width), bf16),
        grid=(per_home, row_blocks),
        in_specs=[pl.BlockSpec((col_count, 1, 1, sub, B), lambda h, r: (0, h, r, 0, 0))],
        out_specs=pl.BlockSpec((B, piece_width), lambda h, r: (r, h)),
    )(out)
    return (out, left_next[None, None], right_next[None, None])


def solution(mesh):
    in_specs = (
        P("tok", None),
        P("tok", "col"),
        P("tok", None, None),
        P("tok", "col", None, None, None),
        P("tok", "col", None, None, None),
    )
    out_specs = (
        P("tok", "col"),
        P("tok", "col", None, None, None),
        P("tok", "col", None, None, None),
    )
    return jax.shard_map(
        per_device, mesh=mesh, in_specs=in_specs, out_specs=out_specs, check_vma=False
    )
```

```python
import functools

import jax
import jax.numpy as jnp
from jax import lax
from jax.experimental import pallas as pl
from jax.experimental.pallas import tpu as pltpu
from jax.sharding import PartitionSpec as P

B = 512
decay_rate = 0.9
epsilon = 1e-06
f32 = jnp.float32
bf16 = jnp.bfloat16
MESH = pl.DeviceIdType.MESH
VMEM = pl.BlockSpec(memory_space=pltpu.VMEM)
ANY = pl.BlockSpec(memory_space=pl.ANY)
LIMIT = 60 * 1024 * 1024


def mm(a, b):
    return jnp.dot(a.astype(bf16), b.astype(bf16), preferred_element_type=f32)


def gather_kernel(tok_count, col_count, og_ref, act_ref, og_buf, act_buf, sems, local_sems):
    t = lax.axis_index("tok")
    c = lax.axis_index("col")
    core = lax.rem(c, 2)
    chip = c // 2
    chips = col_count // 2
    partner = chip * 2 + 1 - core
    width = act_buf.shape[3]

    barrier = pltpu.get_barrier_semaphore()
    for d in range(1, col_count):
        pl.semaphore_signal(
            barrier, inc=1, device_id=(t, lax.rem(c + d, col_count)), device_id_type=MESH
        )
    for d in range(1, tok_count):
        pl.semaphore_signal(
            barrier, inc=1, device_id=(lax.rem(t + d, tok_count), c), device_id_type=MESH
        )

    def act_piece(to):
        return act_ref.at[c, :, pl.ds(pl.multiple_of(to * width, width), width)]

    own_act = pltpu.make_async_copy(act_piece(t), act_buf.at[t, c], local_sems.at[0])
    own_act.start()
    own_og = pltpu.make_async_copy(og_ref.at[c], og_buf.at[t, c], local_sems.at[1])
    own_og.start()
    pl.semaphore_wait(barrier, col_count + tok_count - 2)

    def remote(src, dst, kind, sent, received, to):
        return pltpu.make_async_remote_copy(
            src_ref=src,
            dst_ref=dst,
            send_sem=sems.at[kind, 0, sent],
            recv_sem=sems.at[kind, 1, received],
            device_id=to,
            device_id_type=MESH,
        )

    sent = []
    for d in range(1, tok_count):
        to = lax.rem(t + d, tok_count)
        copy = remote(act_piece(to), act_buf.at[t, c], 0, d, t, (to, c))
        copy.start()
        sent.append(copy)
    for d in range(1, col_count):
        to = lax.rem(c + d, col_count)
        copy = remote(og_ref.at[to], og_buf.at[t, c], 1, d, c, (t, to))
        copy.start()
        sent.append(copy)

    for d in range(1, col_count):
        source = lax.rem(c + d, col_count)
        remote(og_buf.at[t, source], og_buf.at[t, source], 1, d, source, (t, source)).wait_recv()
    own_og.wait()

    def pass_on(origin, step, kind):
        to = t + step
        return remote(og_buf.at[origin], og_buf.at[origin], kind, origin, origin, (to, c))

    @pl.when(t < tok_count - 1)
    def _():
        pass_on(t, 1, 2).start()

    @pl.when(t > 0)
    def _():
        pass_on(t, -1, 3).start()

    own_act.wait()
    for d in range(1, tok_count):
        source = lax.rem(t + d, tok_count)
        remote(act_buf.at[source, c], act_buf.at[source, c], 0, d, source, (source, c)).wait_recv()

    def share(piece, kind, sem_sent, sem_received, to):
        return remote(
            act_buf.at[:, piece], act_buf.at[:, piece], kind, sem_sent, sem_received, (t, to)
        )

    for d in range(1, chips):
        to = lax.rem(chip + d, chips) * 2 + core
        copy = share(c, 4, d, chip, to)
        copy.start()
        sent.append(copy)
    copy = share(c, 5, 0, chip, partner)
    copy.start()
    sent.append(copy)

    def relay(origin, step, kind):
        pass_on(origin, -step, kind).wait_recv()

        @pl.when((t + step >= 0) & (t + step < tok_count))
        def _():
            pass_on(origin, step, kind).start()

    for d in range(1, chips):
        other = lax.rem(chip + d, chips)
        piece = other * 2 + core
        share(piece, 4, d, other, piece).wait_recv()
        copy = share(piece, 5, d, other, partner)
        copy.start()
        sent.append(copy)

    for d in range(1, tok_count):

        @pl.when(t - d >= 0)
        def _():
            relay(t - d, 1, 2)

        @pl.when(t + d < tok_count)
        def _():
            relay(t + d, -1, 3)

    for d in range(chips):
        other = lax.rem(chip + d, chips)
        piece = other * 2 + 1 - core
        share(piece, 5, d, other, partner).wait_recv()
    for copy in sent:
        copy.wait_send()
    for origin in range(tok_count):

        @pl.when((t >= origin) & (t < tok_count - 1))
        def _():
            pass_on(origin, 1, 2).wait_send()

        @pl.when((t <= origin) & (t > 0))
        def _():
            pass_on(origin, -1, 3).wait_send()


def grad_kernel(table, og_ref, act_ref, send_ref, grad, *, slots, row_blocks, col_count):
    tok_count = og_ref.shape[0]
    col_blocks, part = grad.shape[1:3]
    base = lax.axis_index("tok") * (row_blocks * col_blocks)
    step = 256
    blocks = step // part

    @pl.loop(0, col_blocks // blocks)
    def _(i):
        rows = pl.ds(pl.multiple_of(i * step, step), step)
        total = sum(
            jnp.dot(og_ref[t, rows], act_ref[t], preferred_element_type=f32)
            for t in range(tok_count)
        ).astype(bf16)
        for r in range(row_blocks):
            grad[r, pl.ds(i * blocks, blocks)] = total[:, r * B : (r + 1) * B].reshape(
                blocks, part, B
            )

    @pl.loop(0, col_count)
    def _(o):
        for s in range(slots):
            owned = table[o * slots + s]
            place = jnp.maximum(owned - base, 0)
            piece = grad[place // col_blocks, lax.rem(place, col_blocks)]
            send_ref[o, s] = jnp.where(owned >= 0, piece, jnp.zeros_like(piece))


def root_minus_identity(matrix, diagonal):
    side = matrix.shape[-1]
    scale = 0.25 * side / jnp.sum(jnp.where(diagonal, matrix, 0.0))
    e = jnp.where(diagonal, 0.25, 0.0) - matrix * scale
    eb = e.astype(bf16)
    w = 2.0 * e + mm(eb, eb)
    v = w + e + mm(eb, w)
    r = v - 1.25 * w
    return (1.25 * e + r - 0.25 * v + mm(v, r)).astype(bf16)


def slot_math(gt, left_old, right_old, decay):
    g = gt.T
    rows = lax.broadcasted_iota(jnp.int32, (B, B), 0)
    cols = lax.broadcasted_iota(jnp.int32, (B, B), 1)
    diagonal = rows == cols
    left = decay * left_old + jnp.dot(g, gt, preferred_element_type=f32)
    right = decay * right_old + jnp.dot(gt, g, preferred_element_type=f32)
    yl = root_minus_identity(left, diagonal)
    yr = root_minus_identity(right, diagonal)
    g32 = gt.astype(f32)
    first = g32 + jnp.dot(yr, gt, preferred_element_type=f32)
    shaped = first + mm(first, yl)
    grad_norm = jnp.sqrt(jnp.sum(g32 * g32, keepdims=True) + epsilon)
    shaped_norm = jnp.sqrt(jnp.sum(shaped * shaped, keepdims=True) + epsilon)
    return (shaped * (grad_norm / shaped_norm)).astype(bf16), left, right


def block_kernel(
    slots,
    per_home,
    decay_ref,
    pick_ref,
    send_ref,
    left_ref,
    right_ref,
    home_ref,
    left_out,
    right_out,
    grams,
    got,
    back,
    returned,
    leaving,
    sems,
    local_sems,
):
    t = lax.axis_index("tok")
    c = lax.axis_index("col")
    per_block, col_count = got.shape[1:3]
    row_blocks = home_ref.shape[2]
    others = [lax.rem(c + d, col_count) for d in range(1, col_count)]

    barrier = pltpu.get_barrier_semaphore()
    for other in others:
        pl.semaphore_signal(barrier, inc=1, device_id=(t, other), device_id_type=MESH)

    def load(side, s):
        source = (left_ref, right_ref)[side]
        return pltpu.make_async_copy(source.at[s], grams.at[side, s], local_sems.at[side, s])

    def store(side, s):
        target = (left_out, right_out)[side]
        return pltpu.make_async_copy(grams.at[side, s], target.at[s], local_sems.at[side, s])

    def keep(s):
        return pltpu.make_async_copy(send_ref.at[c, s], got.at[s, :, c], local_sems.at[2, s])

    def keep_back(s):
        return pltpu.make_async_copy(
            back.at[s, :, c], returned.at[c * slots + s], local_sems.at[3, s]
        )

    keep_home = pltpu.make_async_copy(leaving.at[c], home_ref.at[c], local_sems.at[4, 0])

    def remote(src, dst, kind, sent, received, to):
        return pltpu.make_async_remote_copy(
            src_ref=src,
            dst_ref=dst,
            send_sem=sems.at[kind, 0, sent],
            recv_sem=sems.at[kind, 1, received],
            device_id=(t, to),
            device_id_type=MESH,
        )

    def out_copy(s, place, to):
        return remote(send_ref.at[to, s], got.at[s, :, place], s, to, place, to)

    def back_copy(s, place, to):
        return remote(
            back.at[s, :, to], returned.at[place * slots + s], slots + s, to, place, to
        )

    def home_copy(place, to):
        return remote(leaving.at[to], home_ref.at[place], 2 * slots, to, place, to)

    for s in range(slots):
        load(0, s).start()
        load(1, s).start()
        keep(s).start()
    pl.semaphore_wait(barrier, col_count - 1)

    @pl.loop(0, slots)
    def _(s):
        for other in others:
            out_copy(s, c, other).start()

    @pl.loop(0, slots)
    def _(s):
        keep(s).wait()
        load(0, s).wait()
        load(1, s).wait()
        for other in others:
            out_copy(s, other, other).wait_recv()
        result, left, right = slot_math(
            got[s].reshape(B, B), grams[0, s], grams[1, s], decay_ref[s]
        )
        back[s] = result.reshape(back.shape[1:])
        grams[0, s] = left
        grams[1, s] = right
        for other in others:
            back_copy(s, c, other).start()
        keep_back(s).start()
        store(0, s).start()
        store(1, s).start()

    @pl.loop(0, slots)
    def _(s):
        keep_back(s).wait()
        for other in others:
            back_copy(s, other, other).wait_recv()

    @pl.loop(0, col_count)
    def _(h):
        for p in range(per_home):
            home = h * per_home + p
            for r in range(row_blocks):
                place = pick_ref[(home // per_block) * row_blocks + r]
                leaving[h, p, r] = returned[place, lax.rem(home, per_block)]

    for other in others:
        home_copy(c, other).start()
    keep_home.start()

    @pl.loop(0, slots)
    def _(s):
        for other in others:
            out_copy(s, c, other).wait_send()
            back_copy(s, c, other).wait_send()
        store(0, s).wait()
        store(1, s).wait()

    keep_home.wait()
    for other in others:
        home_copy(other, other).wait_recv()
        home_copy(c, other).wait_send()


def place_kernel(in_ref, out_ref):
    width = out_ref.shape[1]
    out_ref[...] = in_ref[...].reshape(width, B).T


def per_device(activations, out_grad, owned_blocks, gram_left, gram_right):
    tok_count = lax.axis_size("tok")
    col_count = lax.axis_size("col")
    tok_index = lax.axis_index("tok")
    col_index = lax.axis_index("col")
    tok_local, shard_width = out_grad.shape
    rows_home = activations.shape[1] // tok_count
    row_blocks = rows_home // B
    col_blocks = shard_width * col_count // B
    piece_width = min(B, shard_width)
    per_home = shard_width // piece_width
    per_block = B // piece_width
    sub = piece_width // col_count
    part = per_block * sub
    owners = owned_blocks[0]
    slots = owners.shape[1]

    og = out_grad.T.reshape(per_home, col_count, sub, tok_local).transpose(1, 0, 2, 3)
    og = og.reshape(col_count, per_home * sub, tok_local)
    act = activations.reshape(col_count, tok_local // col_count, activations.shape[1])
    og, act = pl.pallas_call(
        functools.partial(gather_kernel, tok_count, col_count),
        out_shape=[
            jax.ShapeDtypeStruct((tok_count, col_count, per_home * sub, tok_local), bf16),
            jax.ShapeDtypeStruct(
                (tok_count, col_count, tok_local // col_count, rows_home), bf16
            ),
        ],
        in_specs=[ANY, ANY],
        out_specs=[VMEM, VMEM],
        scratch_shapes=[
            pltpu.SemaphoreType.DMA((6, 2, max(col_count, tok_count))),
            pltpu.SemaphoreType.DMA((2,)),
        ],
        compiler_params=pltpu.CompilerParams(
            collective_id=0, has_side_effects=True, vmem_limit_bytes=LIMIT // 4
        ),
    )(og, act)
    og = og.reshape(tok_count, col_count * per_home * sub, tok_local)
    act = act.reshape(tok_count, tok_local, rows_home)

    send = pl.pallas_call(
        functools.partial(
            grad_kernel, slots=slots, row_blocks=row_blocks, col_count=col_count
        ),
        out_shape=jax.ShapeDtypeStruct((col_count, slots, part, B), bf16),
        in_specs=[pl.BlockSpec(memory_space=pltpu.SMEM), VMEM, VMEM],
        out_specs=VMEM,
        scratch_shapes=[pltpu.VMEM((row_blocks, col_blocks, part, B), bf16)],
        compiler_params=pltpu.CompilerParams(vmem_limit_bytes=LIMIT // 2),
    )(owners.reshape(-1), og, act)
    send = send.reshape(col_count, slots, per_block, sub, B)

    mine = lax.dynamic_index_in_dim(owners, col_index, 0, keepdims=False) >= 0
    decays = jnp.where(mine, decay_rate, 1.0).astype(f32)
    wanted = (tok_index * row_blocks + jnp.arange(row_blocks))[None, :] * col_blocks + (
        jnp.arange(col_blocks)
    )[:, None]
    match = owners.reshape(-1)[None, None, :] == wanted[:, :, None]
    pick = jnp.argmax(match, axis=2).astype(jnp.int32).reshape(-1)
    smem = pl.BlockSpec(memory_space=pltpu.SMEM)
    out, left_next, right_next = pl.pallas_call(
        functools.partial(block_kernel, slots, per_home),
        out_shape=[
            jax.ShapeDtypeStruct((col_count, per_home, row_blocks, sub, B), bf16),
            jax.ShapeDtypeStruct((slots, B, B), f32),
            jax.ShapeDtypeStruct((slots, B, B), f32),
        ],
        in_specs=[smem, smem, ANY, ANY, ANY],
        out_specs=[VMEM, ANY, ANY],
        scratch_shapes=[
            pltpu.VMEM((2, slots, B, B), f32),
            pltpu.VMEM((slots, per_block, col_count, sub, B), bf16),
            pltpu.VMEM((slots, per_block, col_count, sub, B), bf16),
            pltpu.VMEM((col_count * slots, per_block, sub, B), bf16),
            pltpu.VMEM((col_count, per_home, row_blocks, sub, B), bf16),
            pltpu.SemaphoreType.DMA((2 * slots + 1, 2, col_count)),
            pltpu.SemaphoreType.DMA((5, slots)),
        ],
        compiler_params=pltpu.CompilerParams(
            collective_id=1, has_side_effects=True, vmem_limit_bytes=LIMIT
        ),
    )(decays, pick, send, gram_left[0, 0], gram_right[0, 0])
    out = pl.pallas_call(
        place_kernel,
        out_shape=jax.ShapeDtypeStruct((rows_home, shard_width), bf16),
        grid=(per_home, row_blocks),
        in_specs=[pl.BlockSpec((col_count, 1, 1, sub, B), lambda h, r: (0, h, r, 0, 0))],
        out_specs=pl.BlockSpec((B, piece_width), lambda h, r: (r, h)),
    )(out)
    return (out, left_next[None, None], right_next[None, None])


def solution(mesh):
    in_specs = (
        P("tok", None),
        P("tok", "col"),
        P("tok", None, None),
        P("tok", "col", None, None, None),
        P("tok", "col", None, None, None),
    )
    out_specs = (
        P("tok", "col"),
        P("tok", "col", None, None, None),
        P("tok", "col", None, None, None),
    )
    return jax.shard_map(
        per_device, mesh=mesh, in_specs=in_specs, out_specs=out_specs, check_vma=False
    )
```

```python
import functools

import jax
import jax.numpy as jnp
from jax import lax
from jax.experimental import pallas as pl
from jax.experimental.pallas import tpu as pltpu
from jax.sharding import PartitionSpec as P

B = 512
decay_rate = 0.9
epsilon = 1e-06
f32 = jnp.float32
bf16 = jnp.bfloat16
MESH = pl.DeviceIdType.MESH
VMEM = pl.BlockSpec(memory_space=pltpu.VMEM)
ANY = pl.BlockSpec(memory_space=pl.ANY)
MIB = 1024 * 1024


def mm(a, b):
    return jnp.dot(a.astype(bf16), b.astype(bf16), preferred_element_type=f32)


def gather_kernel(tok_count, col_count, og_ref, act_ref, og_buf, act_buf, sems, local_sems):
    t = lax.axis_index("tok")
    c = lax.axis_index("col")
    core = lax.rem(c, 2)
    chip = c // 2
    chips = col_count // 2
    partner = chip * 2 + 1 - core
    width = act_buf.shape[3]

    barrier = pltpu.get_barrier_semaphore()
    for d in range(1, col_count):
        pl.semaphore_signal(
            barrier, inc=1, device_id=(t, lax.rem(c + d, col_count)), device_id_type=MESH
        )
    for d in range(1, tok_count):
        pl.semaphore_signal(
            barrier, inc=1, device_id=(lax.rem(t + d, tok_count), c), device_id_type=MESH
        )

    def act_piece(to):
        return act_ref.at[c, :, pl.ds(pl.multiple_of(to * width, width), width)]

    own_act = pltpu.make_async_copy(act_piece(t), act_buf.at[t, c], local_sems.at[0])
    own_act.start()
    own_og = pltpu.make_async_copy(og_ref.at[c], og_buf.at[t, c], local_sems.at[1])
    own_og.start()
    pl.semaphore_wait(barrier, col_count + tok_count - 2)

    def remote(src, dst, kind, sent, received, to):
        return pltpu.make_async_remote_copy(
            src_ref=src,
            dst_ref=dst,
            send_sem=sems.at[kind, 0, sent],
            recv_sem=sems.at[kind, 1, received],
            device_id=to,
            device_id_type=MESH,
        )

    sent = []
    for d in range(1, tok_count):
        to = lax.rem(t + d, tok_count)
        copy = remote(act_piece(to), act_buf.at[t, c], 0, d, t, (to, c))
        copy.start()
        sent.append(copy)
    for d in range(1, col_count):
        to = lax.rem(c + d, col_count)
        copy = remote(og_ref.at[to], og_buf.at[t, c], 1, d, c, (t, to))
        copy.start()
        sent.append(copy)

    for d in range(1, col_count):
        source = lax.rem(c + d, col_count)
        remote(og_buf.at[t, source], og_buf.at[t, source], 1, d, source, (t, source)).wait_recv()
    own_og.wait()

    def pass_on(origin, step, kind):
        to = t + step
        return remote(og_buf.at[origin], og_buf.at[origin], kind, origin, origin, (to, c))

    @pl.when(t < tok_count - 1)
    def _():
        pass_on(t, 1, 2).start()

    @pl.when(t > 0)
    def _():
        pass_on(t, -1, 3).start()

    own_act.wait()
    for d in range(1, tok_count):
        source = lax.rem(t + d, tok_count)
        remote(act_buf.at[source, c], act_buf.at[source, c], 0, d, source, (source, c)).wait_recv()

    def share(piece, kind, sem_sent, sem_received, to):
        return remote(
            act_buf.at[:, piece], act_buf.at[:, piece], kind, sem_sent, sem_received, (t, to)
        )

    for d in range(1, chips):
        to = lax.rem(chip + d, chips) * 2 + core
        copy = share(c, 4, d, chip, to)
        copy.start()
        sent.append(copy)
    copy = share(c, 5, 0, chip, partner)
    copy.start()
    sent.append(copy)

    def relay(origin, step, kind):
        pass_on(origin, -step, kind).wait_recv()

        @pl.when((t + step >= 0) & (t + step < tok_count))
        def _():
            pass_on(origin, step, kind).start()

    for d in range(1, chips):
        other = lax.rem(chip + d, chips)
        piece = other * 2 + core
        share(piece, 4, d, other, piece).wait_recv()
        copy = share(piece, 5, d, other, partner)
        copy.start()
        sent.append(copy)

    for d in range(1, tok_count):

        @pl.when(t - d >= 0)
        def _():
            relay(t - d, 1, 2)

        @pl.when(t + d < tok_count)
        def _():
            relay(t + d, -1, 3)

    for d in range(chips):
        other = lax.rem(chip + d, chips)
        piece = other * 2 + 1 - core
        share(piece, 5, d, other, partner).wait_recv()
    for copy in sent:
        copy.wait_send()
    for origin in range(tok_count):

        @pl.when((t >= origin) & (t < tok_count - 1))
        def _():
            pass_on(origin, 1, 2).wait_send()

        @pl.when((t <= origin) & (t > 0))
        def _():
            pass_on(origin, -1, 3).wait_send()


def grad_kernel(
    table, og_ref, act_ref, send_ref, pick_ref, decay_ref, grad, *, slots, row_blocks, col_count
):
    tok_count = og_ref.shape[0]
    col_blocks, part = grad.shape[1:3]
    base = lax.axis_index("tok") * (row_blocks * col_blocks)
    step = 256
    blocks = step // part

    @pl.loop(0, col_blocks // blocks)
    def _(i):
        rows = pl.ds(pl.multiple_of(i * step, step), step)
        total = sum(
            jnp.dot(og_ref[t, rows], act_ref[t], preferred_element_type=f32)
            for t in range(tok_count)
        ).astype(bf16)
        for r in range(row_blocks):
            grad[r, pl.ds(i * blocks, blocks)] = total[:, r * B : (r + 1) * B].reshape(
                blocks, part, B
            )

    mine = lax.axis_index("col") * slots
    for s in range(slots):
        decay_ref[s] = jnp.where(table[mine + s] >= 0, f32(decay_rate), f32(1.0))

    @pl.loop(0, col_count)
    def _(o):
        for s in range(slots):
            owned = table[o * slots + s]
            place = jnp.maximum(owned - base, 0)
            piece = grad[place // col_blocks, lax.rem(place, col_blocks)]
            send_ref[o, s] = jnp.where(owned >= 0, piece, jnp.zeros_like(piece))
            pick_ref[jnp.where(owned >= 0, place, row_blocks * col_blocks)] = o * slots + s


def root_minus_identity(matrix, diagonal):
    side = matrix.shape[-1]
    scale = 0.25 * side / jnp.sum(jnp.where(diagonal, matrix, 0.0))
    e = jnp.where(diagonal, 0.25, 0.0) - matrix * scale
    eb = e.astype(bf16)
    w = 2.0 * e + mm(eb, eb)
    v = w + e + mm(eb, w)
    r = v - 1.25 * w
    return (1.25 * e + r - 0.25 * v + mm(v, r)).astype(bf16)


def slot_math(gt, left_old, right_old, decay):
    g = gt.T
    rows = lax.broadcasted_iota(jnp.int32, (B, B), 0)
    cols = lax.broadcasted_iota(jnp.int32, (B, B), 1)
    diagonal = rows == cols
    left = decay * left_old + jnp.dot(g, gt, preferred_element_type=f32)
    right = decay * right_old + jnp.dot(gt, g, preferred_element_type=f32)
    yl = root_minus_identity(left, diagonal)
    yr = root_minus_identity(right, diagonal)
    g32 = gt.astype(f32)
    first = g32 + jnp.dot(yr, gt, preferred_element_type=f32)
    shaped = first + mm(first, yl)
    grad_norm = jnp.sqrt(jnp.sum(g32 * g32, keepdims=True) + epsilon)
    shaped_norm = jnp.sqrt(jnp.sum(shaped * shaped, keepdims=True) + epsilon)
    return (shaped * (grad_norm / shaped_norm)).astype(bf16), left, right


def block_kernel(
    slots,
    per_home,
    decay_ref,
    pick_ref,
    send_ref,
    left_ref,
    right_ref,
    home_ref,
    left_out,
    right_out,
    got,
    back,
    returned,
    leaving,
    sems,
    local_sems,
):
    t = lax.axis_index("tok")
    c = lax.axis_index("col")
    per_block, col_count = got.shape[1:3]
    row_blocks = home_ref.shape[2]
    col_blocks = col_count * per_home // per_block
    others = [lax.rem(c + d, col_count) for d in range(1, col_count)]

    barrier = pltpu.get_barrier_semaphore()
    for other in others:
        pl.semaphore_signal(barrier, inc=1, device_id=(t, other), device_id_type=MESH)

    def load(side, s):
        source = (left_ref, right_ref)[side]
        target = (left_out, right_out)[side]
        return pltpu.make_async_copy(source.at[s], target.at[s], local_sems.at[side, s])

    def keep(s):
        return pltpu.make_async_copy(send_ref.at[c, s], got.at[s, :, c], local_sems.at[2, s])

    def keep_back(s):
        return pltpu.make_async_copy(
            back.at[s, :, c], returned.at[c * slots + s], local_sems.at[3, s]
        )

    keep_home = pltpu.make_async_copy(leaving.at[c], home_ref.at[c], local_sems.at[4, 0])

    def remote(src, dst, kind, sent, received, to):
        return pltpu.make_async_remote_copy(
            src_ref=src,
            dst_ref=dst,
            send_sem=sems.at[kind, 0, sent],
            recv_sem=sems.at[kind, 1, received],
            device_id=(t, to),
            device_id_type=MESH,
        )

    def out_copy(s, place, to):
        return remote(send_ref.at[to, s], got.at[s, :, place], s, to, place, to)

    def back_copy(s, place, to):
        return remote(
            back.at[s, :, to], returned.at[place * slots + s], slots + s, to, place, to
        )

    def home_copy(place, to):
        return remote(leaving.at[to], home_ref.at[place], 2 * slots, to, place, to)

    for s in range(slots):
        load(0, s).start()
        load(1, s).start()
        keep(s).start()
    pl.semaphore_wait(barrier, col_count - 1)

    @pl.loop(0, slots)
    def _(s):
        for other in others:
            out_copy(s, c, other).start()

    @pl.loop(0, slots)
    def _(s):
        keep(s).wait()
        load(0, s).wait()
        load(1, s).wait()
        for other in others:
            out_copy(s, other, other).wait_recv()
        result, left, right = slot_math(
            got[s].reshape(B, B), left_out[s], right_out[s], decay_ref[s]
        )
        back[s] = result.reshape(back.shape[1:])
        left_out[s] = left
        right_out[s] = right
        for other in others:
            back_copy(s, c, other).start()
        keep_back(s).start()

    @pl.loop(0, slots)
    def _(s):
        keep_back(s).wait()
        for other in others:
            back_copy(s, other, other).wait_recv()

    @pl.loop(0, col_count)
    def _(h):
        for p in range(per_home):
            home = h * per_home + p
            for r in range(row_blocks):
                place = pick_ref[r * col_blocks + home // per_block]
                leaving[h, p, r] = returned[place, lax.rem(home, per_block)]

    for other in others:
        home_copy(c, other).start()
    keep_home.start()

    @pl.loop(0, slots)
    def _(s):
        for other in others:
            out_copy(s, c, other).wait_send()
            back_copy(s, c, other).wait_send()

    keep_home.wait()
    for other in others:
        home_copy(other, other).wait_recv()
        home_copy(c, other).wait_send()


def place_kernel(in_ref, left_ref, right_ref, out_ref, left_out, right_out, tiles, sems):
    per_home, row_blocks, _, width = tiles.shape
    copies = [
        pltpu.make_async_copy(left_ref, left_out, sems.at[0]),
        pltpu.make_async_copy(right_ref, right_out, sems.at[1]),
    ]
    for copy in copies:
        copy.start()
    for h in range(per_home):
        for r in range(row_blocks):
            tiles[h, r] = in_ref[:, h, r].reshape(width, B).T
            copy = pltpu.make_async_copy(
                tiles.at[h, r],
                out_ref.at[pl.ds(r * B, B), pl.ds(h * width, width)],
                sems.at[len(copies)],
            )
            copy.start()
            copies.append(copy)
    for copy in copies:
        copy.wait()


def per_device(activations, out_grad, owned_blocks, gram_left, gram_right):
    tok_count = lax.axis_size("tok")
    col_count = lax.axis_size("col")
    tok_index = lax.axis_index("tok")
    col_index = lax.axis_index("col")
    tok_local, shard_width = out_grad.shape
    rows_home = activations.shape[1] // tok_count
    row_blocks = rows_home // B
    col_blocks = shard_width * col_count // B
    piece_width = min(B, shard_width)
    per_home = shard_width // piece_width
    per_block = B // piece_width
    sub = piece_width // col_count
    part = per_block * sub
    owners = owned_blocks[0]
    slots = owners.shape[1]

    og = out_grad.T.reshape(per_home, col_count, sub, tok_local).transpose(1, 0, 2, 3)
    og = og.reshape(col_count, per_home * sub, tok_local)
    act = activations.reshape(col_count, tok_local // col_count, activations.shape[1])
    og, act = pl.pallas_call(
        functools.partial(gather_kernel, tok_count, col_count),
        out_shape=[
            jax.ShapeDtypeStruct((tok_count, col_count, per_home * sub, tok_local), bf16),
            jax.ShapeDtypeStruct(
                (tok_count, col_count, tok_local // col_count, rows_home), bf16
            ),
        ],
        in_specs=[ANY, ANY],
        out_specs=[VMEM, VMEM],
        scratch_shapes=[
            pltpu.SemaphoreType.DMA((6, 2, max(col_count, tok_count))),
            pltpu.SemaphoreType.DMA((2,)),
        ],
        compiler_params=pltpu.CompilerParams(
            collective_id=0, has_side_effects=True, vmem_limit_bytes=15 * MIB
        ),
    )(og, act)
    og = og.reshape(tok_count, col_count * per_home * sub, tok_local)
    act = act.reshape(tok_count, tok_local, rows_home)

    smem = pl.BlockSpec(memory_space=pltpu.SMEM)
    send, pick, decays = pl.pallas_call(
        functools.partial(
            grad_kernel, slots=slots, row_blocks=row_blocks, col_count=col_count
        ),
        out_shape=[
            jax.ShapeDtypeStruct((col_count, slots, part, B), bf16),
            jax.ShapeDtypeStruct((row_blocks * col_blocks + 1,), jnp.int32),
            jax.ShapeDtypeStruct((slots,), f32),
        ],
        in_specs=[smem, VMEM, VMEM],
        out_specs=[VMEM, smem, smem],
        scratch_shapes=[pltpu.VMEM((row_blocks, col_blocks, part, B), bf16)],
        compiler_params=pltpu.CompilerParams(vmem_limit_bytes=30 * MIB),
    )(owners.reshape(-1), og, act)
    send = send.reshape(col_count, slots, per_block, sub, B)

    out, left_next, right_next = pl.pallas_call(
        functools.partial(block_kernel, slots, per_home),
        out_shape=[
            jax.ShapeDtypeStruct((col_count, per_home, row_blocks, sub, B), bf16),
            jax.ShapeDtypeStruct((slots, B, B), f32),
            jax.ShapeDtypeStruct((slots, B, B), f32),
        ],
        in_specs=[smem, smem, ANY, ANY, ANY],
        out_specs=[VMEM, VMEM, VMEM],
        scratch_shapes=[
            pltpu.VMEM((slots, per_block, col_count, sub, B), bf16),
            pltpu.VMEM((slots, per_block, col_count, sub, B), bf16),
            pltpu.VMEM((col_count * slots, per_block, sub, B), bf16),
            pltpu.VMEM((col_count, per_home, row_blocks, sub, B), bf16),
            pltpu.SemaphoreType.DMA((2 * slots + 1, 2, col_count)),
            pltpu.SemaphoreType.DMA((5, slots)),
        ],
        compiler_params=pltpu.CompilerParams(
            collective_id=1, has_side_effects=True, vmem_limit_bytes=30 * MIB
        ),
    )(decays, pick, send, gram_left[0, 0], gram_right[0, 0])
    return tuple(
        pl.pallas_call(
            place_kernel,
            out_shape=[
                jax.ShapeDtypeStruct((rows_home, shard_width), bf16),
                jax.ShapeDtypeStruct((1, 1, slots, B, B), f32),
                jax.ShapeDtypeStruct((1, 1, slots, B, B), f32),
            ],
            in_specs=[VMEM, VMEM, VMEM],
            out_specs=[ANY, ANY, ANY],
            scratch_shapes=[
                pltpu.VMEM((per_home, row_blocks, B, piece_width), bf16),
                pltpu.SemaphoreType.DMA((2 + per_home * row_blocks,)),
            ],
            compiler_params=pltpu.CompilerParams(vmem_limit_bytes=16 * MIB),
        )(out, left_next[None, None], right_next[None, None])
    )


def solution(mesh):
    in_specs = (
        P("tok", None),
        P("tok", "col"),
        P("tok", None, None),
        P("tok", "col", None, None, None),
        P("tok", "col", None, None, None),
    )
    out_specs = (
        P("tok", "col"),
        P("tok", "col", None, None, None),
        P("tok", "col", None, None, None),
    )
    return jax.shard_map(
        per_device, mesh=mesh, in_specs=in_specs, out_specs=out_specs, check_vma=False
    )
```
